128 devices in a mesh: ctx: 16 (over y, z_hi, core), ch: 2 (over z_lo), dp: 4 (over x).
Axes of the slice: x: 4, y: 4, z: 4 (z_hi: 2, z_lo: 2; z = z_hi * 2 + z_lo), core: 2. Of those that a mesh axis runs over, the one named last changes fastest.
Arguments:
- features: bfloat16 [32768, 3, 4096], P(('dp', 'ctx'), None, 'ch'), parts along dimension 0, may hold values from -6 to 6
- short_filter: float32 [3, 3, 4096], P(None, None, 'ch'), may hold values from -3.5 to 3.5
- mode_residue: float32 [16, 4096], P(None, 'ch'), may hold values from -0.18 to 0.18
- decay_mix: float32 [16, 4096], P(None, 'ch'), may hold values from 0 to 1
- skip_gain: float32 [4096], P('ch'), may hold values from 0.5 to 1.5
- counter: int32 [8], P('dp'), parts along dimension 0, may hold values from 0 to 1048575
- out_weight: bfloat16 [4096, 4096], P('ch'), may hold values from -0.09375 to 0.09375
Outputs:
- projected: bfloat16 [32768, 4096], P(('dp', 'ctx', 'ch')), parts along dimension 0
The draws below stay inside these ranges and needn't reach their ends.
There are 4 independent parts, one for each index of `dp`. The reference program is written for one: setup_inputs(seed, part) draws one part's arguments, and reference() takes and returns one part's arrays. A program takes and returns all parts, laid end to end along the dimension named above; an argument that names none is the same for every part. Nothing has to cross between parts.
All inputs are finite; a program needn't handle non-finite values.
Results may differ from the reference program's by a relative error of at most 0.012.
Values may be sent and summed in bfloat16 or wider, within the bound.
No kernel may reach another device: no remote copies, remote signals or barrier semaphores. Data moves between devices by JAX's collectives and lax.ppermute only.
A program may use at most 256 MiB of HBM per device.

```python
import math
import jax
import jax.numpy as jnp
from jax import lax

DW = 4096
DO = 4096
ORD = 16
SHORT = 3
TOKENS = 8192


def draw_decay_mix(key, part):
    values = jax.random.uniform(key, (ORD, DW), jnp.float32)
    return values


def shard_levels(own_key, extent, cuts, low, high):
    def one(position, blocks):
        heights = jax.random.uniform(jax.random.fold_in(jax.random.fold_in(own_key, 6), position), (blocks,), jnp.float32, low / len(cuts), high / len(cuts))
        return jnp.repeat(jnp.exp(heights), extent[position] // blocks).reshape((-1,) + (1,) * (len(extent) - position - 1))

    level = one(*cuts[0])
    for cut in cuts[1:]:
        level = level * one(*cut)
    return level


def centred(stream_key, shape, spread, most, split=(), kind=jnp.bfloat16):
    result = spread * jax.random.normal(stream_key, shape, jnp.float32)
    if split:
        result = result * shard_levels(stream_key, shape, split, -0.22, 0.18)
    return jnp.clip(result, -most, most).astype(kind)


def setup_inputs(seed: int = 0, part: int = 0) -> dict:
    keys = jax.random.split(jax.random.key(seed), 8)
    part_keys = jax.random.split(jax.random.fold_in(keys[7], part), 8)
    return {
        "features": centred(part_keys[0], (TOKENS, 3, DW), 1.0, 6.0, ((0, 16), (2, 2))),
        "short_filter": centred(keys[1], (3, SHORT, DW), SHORT ** -0.5, 3.5, ((2, 2),), jnp.float32),
        "mode_residue": centred(keys[2], (ORD, DW), 0.03, 0.18, ((1, 2),), jnp.float32),
        "decay_mix": draw_decay_mix(jax.random.fold_in(keys[7], 71), part),
        "skip_gain": jnp.clip(0.5 + 1.0 * jax.random.uniform(keys[4], (DW,), jnp.float32) ** shard_levels(keys[4], (DW,), ((0, 2),), -0.2, 0.2), 0.5, 1.5),
        "counter": jax.random.randint(part_keys[5], (2,), 0, 1048576).astype(jnp.int32),
        "out_weight": centred(keys[6], (DW, DO), DW ** -0.5, 0.09375, ((0, 2),)),
    }


keep_scale = 8.0 / 7.0


def keep_mask(hash_base, positions, channels):
    bits = hash_base + positions[:, None] * jnp.int32(-1640531535) + channels[None, :] * jnp.int32(-2048144777)
    bits = bits ^ lax.shift_right_logical(bits, jnp.full_like(bits, 16))
    bits = bits * jnp.int32(2146121005)
    bits = bits ^ lax.shift_right_logical(bits, jnp.full_like(bits, 15))
    bits = bits * jnp.int32(-2073254261)
    bits = bits ^ lax.shift_right_logical(bits, jnp.full_like(bits, 16))
    return lax.shift_right_logical(bits, jnp.full_like(bits, 29)) != 0


def rates_of(mix, length):
    return jnp.exp(-((1.0 - mix) * math.log(length) + mix * math.log(30.0)))


def build_filter(residue, mix, length):
    rates = rates_of(mix, length)
    times = jnp.arange(length, dtype=jnp.int32).astype(jnp.float32)

    def add_mode(order_index, total):
        return total + residue[order_index][None, :] * jnp.exp(-rates[order_index][None, :] * times[:, None])

    return lax.fori_loop(0, residue.shape[0], add_mode, jnp.zeros((length, residue.shape[1]), jnp.float32))


def reference(features, short_filter, mode_residue, decay_mix, skip_gain, counter, out_weight):
    padded = jnp.concatenate([jnp.zeros((SHORT - 1, 3, DW), jnp.bfloat16), features], axis=0).astype(jnp.float32)
    filtered = jnp.zeros((TOKENS, 3, DW), jnp.float32)
    for lag in range(SHORT):
        filtered = filtered + short_filter[:, lag, :][None] * padded[SHORT - 1 - lag:SHORT - 1 - lag + TOKENS]
    query = filtered[:, 0]
    keyed = filtered[:, 1]
    valued = filtered[:, 2]
    positions = counter[1] + jnp.arange(TOKENS, dtype=jnp.int32)
    channels = jnp.arange(DW, dtype=jnp.int32)
    gated = jnp.where(keep_mask(counter[0], positions, channels), keyed * valued * keep_scale, 0.0).astype(jnp.bfloat16)
    gated_wide = gated.astype(jnp.float32)
    long_filter = build_filter(mode_residue, decay_mix, TOKENS)
    total_len = 2 * TOKENS
    spectrum = jnp.fft.rfft(gated_wide, n=total_len, axis=0) * jnp.fft.rfft(long_filter, n=total_len, axis=0)
    convolved = jnp.fft.irfft(spectrum, n=total_len, axis=0)[:TOKENS]
    long_out = convolved + skip_gain[None, :] * gated_wide
    mixed = (query * long_out).astype(jnp.bfloat16)
    return jnp.dot(mixed, out_weight, preferred_element_type=jnp.float32).astype(jnp.bfloat16)
```

```python
import math

import jax
import jax.numpy as jnp
from jax import lax
from jax.experimental import pallas as pl
from jax.experimental.pallas import tpu as pltpu
from jax.sharding import PartitionSpec as P

SHORT = 3
ORDER = 16
LANES = 128
SUBS = 8
KEEP_SCALE = 8.0 / 7.0
COL_CHUNKS = 4


def rates_of(mix, length):
    return jnp.exp(-((1.0 - mix) * math.log(length) + mix * math.log(30.0)))


def row(table, index):
    return jnp.broadcast_to(table[index : index + 1, :], (SUBS, table.shape[1]))


def gate_kernel(tokens, half, step_rows, width, info, key_ref, value_ref, edge_ref, taps_ref, mix_ref,
                gated_ref, start_ref, end_ref, key_rows, value_rows):
    block = pl.program_id(0)
    lane = lax.broadcasted_iota(jnp.int32, (SUBS, LANES), 1)
    sub = lax.broadcasted_iota(jnp.int32, (SUBS, LANES), 0)
    for group in range(width // LANES):
        cols = slice(group * LANES, (group + 1) * LANES)
        key_rows[SUBS:, :] = key_ref[:, cols].astype(jnp.float32)
        value_rows[SUBS:, :] = value_ref[:, cols].astype(jnp.float32)
        key_rows[SUBS - 2 : SUBS, :] = edge_ref[0, :, cols]
        value_rows[SUBS - 2 : SUBS, :] = edge_ref[1, :, cols]
        taps = taps_ref[:, cols]
        key_taps = [row(taps, 3 + lag) * KEEP_SCALE for lag in range(SHORT)]
        value_taps = [row(taps, 6 + lag) for lag in range(SHORT)]
        rates = rates_of(mix_ref[:, cols], tokens)
        decay = jnp.exp(-rates)
        decays = [row(decay, r) for r in range(ORDER)]
        channel = info[2] + block * width + group * LANES + lane
        carried = None
        for part in range(2):
            base = SUBS + part * half
            first = info[1] + part * half + sub * step_rows
            bits = info[0] + first * jnp.int32(-1640531535) + channel * jnp.int32(-2048144777)

            def load(rows, at):
                return rows[pl.ds(at, SUBS, stride=step_rows), :]

            def pair(j, carry):
                states, k1, k2, v1, v2, bits = carry
                values = []
                for u in range(2):
                    k0 = load(key_rows, base + 2 * j + u)
                    v0 = load(value_rows, base + 2 * j + u)
                    keyed = key_taps[0] * k0 + key_taps[1] * k1 + key_taps[2] * k2
                    valued = value_taps[0] * v0 + value_taps[1] * v1 + value_taps[2] * v2
                    h = bits
                    h = h ^ lax.shift_right_logical(h, jnp.full_like(h, 16))
                    h = h * jnp.int32(2146121005)
                    h = h ^ lax.shift_right_logical(h, jnp.full_like(h, 15))
                    h = h * jnp.int32(-2073254261)
                    keep = (h & jnp.int32(-536870912)) != 0
                    values.append(jnp.where(keep, keyed * valued, 0.0))
                    k1, k2, v1, v2 = k0, k1, v0, v1
                    bits = bits + jnp.int32(-1640531535)
                rounded = jnp.concatenate(values, axis=0).astype(jnp.bfloat16)
                gated_ref[pl.ds(pl.multiple_of(part * half + j * 2 * SUBS, 2 * SUBS), 2 * SUBS), cols] = rounded
                wide = rounded.astype(jnp.float32)
                g0, g1 = wide[:SUBS], wide[SUBS:]
                states = tuple((x * a + g0) * a + g1 for x, a in zip(states, decays))
                return (states, k1, k2, v1, v2, bits)

            zero = jnp.zeros((SUBS, LANES), jnp.float32)
            init = (
                (zero,) * ORDER,
                load(key_rows, base - 1),
                load(key_rows, base - 2),
                load(value_rows, base - 1),
                load(value_rows, base - 2),
                bits,
            )
            states = lax.fori_loop(0, step_rows // 2, pair, init)[0]
            ends = []
            for r in range(ORDER):
                rate = row(rates, r)
                x = states[r]
                for d in (1, 2, 4):
                    factor = jnp.where(sub >= d, jnp.exp(-rate * float(d * step_rows)), 0.0)
                    x = x + factor * pltpu.roll(x, d, 0)
                before = jnp.where(sub >= 1, pltpu.roll(x, 1, 0), 0.0)
                last = jnp.broadcast_to(x[SUBS - 1 : SUBS, :], (SUBS, LANES))
                if part == 1:
                    before = before + jnp.exp(-rate * (sub * step_rows).astype(jnp.float32)) * carried[r]
                    last = last + jnp.exp(-rate * float(half)) * carried[r]
                    end_ref[r : r + 1, cols] = last[0:1, :]
                start_ref[part, r, :, cols] = before
                ends.append(last)
            carried = ends


def mix_kernel(tokens, half, step_rows, width, info, gated_ref, query_ref, edge_ref, taps_ref, mix_ref, residue_ref,
               skip_ref, start_ref, into_ref, mixed_ref, query_rows, mixed_rows, gains):
    sub = lax.broadcasted_iota(jnp.int32, (SUBS, LANES), 0)
    offset = (info[0] * half + sub * step_rows).astype(jnp.float32)
    for group in range(width // LANES):
        cols = slice(group * LANES, (group + 1) * LANES)
        query_rows[SUBS:, :] = query_ref[:, cols].astype(jnp.float32)
        query_rows[SUBS - 2 : SUBS, :] = edge_ref[0, :, cols]
        taps = taps_ref[:, cols]
        query_taps = [row(taps, lag) for lag in range(SHORT)]
        skip = row(skip_ref[:, cols], 0)
        rates = rates_of(mix_ref[:, cols], tokens)
        decay = jnp.exp(-rates)
        decays = [row(decay, r) for r in range(ORDER)]
        residue = residue_ref[:, cols]
        into = into_ref[:, cols]
        states = []
        for r in range(ORDER):
            gains[r] = row(residue, r)
            states.append(start_ref[0, r, :, cols] + jnp.exp(-row(rates, r) * offset) * row(into, r))

        def load(at):
            return query_rows[pl.ds(at, SUBS, stride=step_rows), :]

        def pair(j, carry):
            states, q1, q2 = carry
            wide = gated_ref[pl.ds(pl.multiple_of(j * 2 * SUBS, 2 * SUBS), 2 * SUBS), cols].astype(jnp.float32)
            for u in range(2):
                g = wide[u * SUBS : (u + 1) * SUBS]
                q0 = load(SUBS + 2 * j + u)
                query = query_taps[0] * q0 + query_taps[1] * q1 + query_taps[2] * q2
                states = tuple(x * a + g for x, a in zip(states, decays))
                terms = [x * gains[r] for r, x in enumerate(states)] + [skip * g]
                while len(terms) > 1:
                    terms = [sum(terms[k : k + 2][1:], terms[k]) for k in range(0, len(terms), 2)]
                mixed_rows[pl.ds(2 * j + u, SUBS, stride=step_rows), :] = query * terms[0]
                q1, q2 = q0, q1
            return (states, q1, q2)

        lax.fori_loop(0, step_rows // 2, pair, (tuple(states), load(SUBS - 1), load(SUBS - 2)))
        mixed_ref[:, cols] = mixed_rows[...].astype(jnp.bfloat16)


def gate(info, planes, edge, taps, mix, tokens):
    rows, channels = planes.shape[1:]
    width = 2 * LANES
    half = rows // 2
    step_rows = half // SUBS
    body = lambda *refs: gate_kernel(tokens, half, step_rows, width, *refs)
    return pl.pallas_call(
        body,
        out_shape=(
            jax.ShapeDtypeStruct((rows, channels), jnp.bfloat16),
            jax.ShapeDtypeStruct((2, ORDER, SUBS, channels), jnp.float32),
            jax.ShapeDtypeStruct((ORDER, channels), jnp.float32),
        ),
        grid_spec=pltpu.PrefetchScalarGridSpec(
            num_scalar_prefetch=1,
            grid=(channels // width,),
            in_specs=[
                pl.BlockSpec((None, rows, width), lambda b, s: (1, 0, b)),
                pl.BlockSpec((None, rows, width), lambda b, s: (2, 0, b)),
                pl.BlockSpec((2, 2, width), lambda b, s: (0, 0, b)),
                pl.BlockSpec((9, width), lambda b, s: (0, b)),
                pl.BlockSpec((ORDER, width), lambda b, s: (0, b)),
            ],
            out_specs=(
                pl.BlockSpec((rows, width), lambda b, s: (0, b)),
                pl.BlockSpec((2, ORDER, SUBS, width), lambda b, s: (0, 0, 0, b)),
                pl.BlockSpec((ORDER, width), lambda b, s: (0, b)),
            ),
            scratch_shapes=[pltpu.VMEM((SUBS + rows, LANES), jnp.float32)] * 2,
        ),
        name="gate",
        cost_estimate=pl.CostEstimate(flops=80 * rows * channels, bytes_accessed=8 * rows * channels, transcendentals=0),
    )(info, planes, planes, edge, taps, mix)


def blend(which, gated, planes, edges, taps, mix, residue, skip, start, into, tokens):
    rows, channels = gated.shape
    width = 2 * LANES
    half = rows // 2
    step_rows = half // SUBS
    body = lambda *refs: mix_kernel(tokens, half, step_rows, width, *refs)
    return pl.pallas_call(
        body,
        out_shape=jax.ShapeDtypeStruct((half, channels), jnp.bfloat16),
        grid_spec=pltpu.PrefetchScalarGridSpec(
            num_scalar_prefetch=1,
            grid=(channels // width,),
            in_specs=[
                pl.BlockSpec((half, width), lambda b, s: (s[0], b)),
                pl.BlockSpec((None, half, width), lambda b, s: (0, s[0], b)),
                pl.BlockSpec((1, 2, width), lambda b, s: (s[0], 0, b)),
                pl.BlockSpec((9, width), lambda b, s: (0, b)),
                pl.BlockSpec((ORDER, width), lambda b, s: (0, b)),
                pl.BlockSpec((ORDER, width), lambda b, s: (0, b)),
                pl.BlockSpec((1, width), lambda b, s: (0, b)),
                pl.BlockSpec((1, ORDER, SUBS, width), lambda b, s: (s[0], 0, 0, b)),
                pl.BlockSpec((ORDER, width), lambda b, s: (0, b)),
            ],
            out_specs=pl.BlockSpec((half, width), lambda b, s: (0, b)),
            scratch_shapes=[
                pltpu.VMEM((SUBS + half, LANES), jnp.float32),
                pltpu.VMEM((half, LANES), jnp.float32),
                pltpu.VMEM((ORDER, SUBS, LANES), jnp.float32),
            ],
        ),
        name="blend",
        cost_estimate=pl.CostEstimate(flops=80 * half * channels, bytes_accessed=8 * half * channels, transcendentals=0),
    )(which, gated, planes, edges, taps, mix, residue, skip, start, into)


def state_before(end, mix, tokens, rows, index, count):
    rates = rates_of(mix, tokens)
    total = end
    into = jnp.zeros_like(end)
    size = 1
    while size < count:
        other = lax.ppermute(total, "ctx", [(i, i ^ size) for i in range(count)])
        upper = (index // size) % 2 == 1
        inside = (index % size).astype(jnp.float32)
        into = into + jnp.where(upper, jnp.exp(-rates * (inside * rows)), 0.0) * other
        across = jnp.exp(-rates * float(rows * size))
        total = jnp.where(upper, across * other + total, across * total + other)
        size *= 2
    return into


def body(features, short_filter, mode_residue, decay_mix, skip_gain, counter, out_weight):
    rows = features.shape[0]
    channels = features.shape[2]
    count = lax.axis_size("ctx")
    tokens = rows * count
    index = lax.axis_index("ctx")
    side = lax.axis_index("ch")
    half = rows // 2
    planes = jnp.transpose(features, (1, 0, 2))
    edge = lax.ppermute(planes[:, rows - (SHORT - 1) :], "ctx", [(i, i + 1) for i in range(count - 1)])
    edge = edge.astype(jnp.float32)
    taps = short_filter.reshape(9, channels)
    info = jnp.stack([counter[0], counter[1] + index * rows, side * channels]).astype(jnp.int32)
    gated, start, end = gate(info, planes, edge[1:], taps, decay_mix, tokens)
    into = state_before(end, decay_mix, tokens, rows, index, count)
    edges = jnp.stack([edge[0], planes[0, half - (SHORT - 1) : half].astype(jnp.float32)])

    def mixed_of(which, after):
        return blend(which.reshape(1), gated, planes, edges, taps, decay_mix, mode_residue, skip_gain[None], start, after, tokens)

    swap = [(0, 1), (1, 0)]
    cols = out_weight.shape[1] // COL_CHUNKS
    sent = mixed_of(1 - side, into)
    received = []
    for c in range(COL_CHUNKS):
        part = jnp.dot(sent, out_weight[:, c * cols : (c + 1) * cols], preferred_element_type=jnp.float32)
        part = part.astype(jnp.bfloat16)
        received.append(lax.ppermute(part, "ch", swap))
    into, part = lax.optimization_barrier((into, part))
    kept = mixed_of(side, into)
    outs = []
    for c in range(COL_CHUNKS):
        part = jnp.dot(kept, out_weight[:, c * cols : (c + 1) * cols], preferred_element_type=jnp.float32)
        outs.append((part + received[c].astype(jnp.float32)).astype(jnp.bfloat16))
    return jnp.concatenate(outs, axis=1)


def solution(mesh):
    placed = (
        P(("dp", "ctx"), None, "ch"),
        P(None, None, "ch"),
        P(None, "ch"),
        P(None, "ch"),
        P("ch"),
        P("dp"),
        P("ch", None),
    )
    return jax.shard_map(
        body, mesh=mesh, in_specs=placed, out_specs=P(("dp", "ctx", "ch"), None), check_vma=False
    )
```

```python
import math

import jax
import jax.numpy as jnp
from jax import lax
from jax.experimental import pallas as pl
from jax.experimental.pallas import tpu as pltpu
from jax.sharding import PartitionSpec as P


SHORT = 3
ORDER = 16
LANES = 128
SUBS = 8
WIDTH = 2 * LANES
KEEP_SCALE = 8.0 / 7.0
SEND_COLS = 512
TILE_COLS = 256
BASE = 40
GAP = 4
QUAD = 4


def rates_of(mix, length):
    return jnp.exp(-((1.0 - mix) * math.log(length) + mix * math.log(30.0)))


def row(table, index):
    return jnp.broadcast_to(table[index : index + 1, :], (SUBS, table.shape[1]))


def spread(rows, source, cols, count, step):
    for n in range(count):
        at = BASE + n * (step + GAP)
        rows[at : at + step, :] = source[n * step : (n + 1) * step, cols].astype(jnp.float32)


def across(rows, at, step):
    return rows[pl.ds(at, SUBS, stride=step + GAP), :]


def lanes_of(block, group):
    return pl.ds(pl.multiple_of(block * WIDTH + group * LANES, LANES), LANES)


def state_of(own_ref, got_ref, core, group):
    blocks = pl.num_programs(0) // 2
    block = pl.program_id(0)
    lanes = lanes_of(block % blocks, group)
    return jnp.where(block // blocks == core, own_ref[:, lanes], got_ref[:, lanes])


def fill(table, values):
    for r in range(ORDER):
        table[r] = row(values, r)


def gate_kernel(tokens, half, step, counter, place, key_ref, value_ref, edge_ref, taps_ref, mix_ref,
                gated_ref, start_ref, mine_ref, other_ref, key_rows, value_rows, decays, taps):
    block = pl.program_id(0)
    lane = lax.broadcasted_iota(jnp.int32, (SUBS, LANES), 1)
    sub = lax.broadcasted_iota(jnp.int32, (SUBS, LANES), 0)
    is_mine = (block * 2) // pl.num_programs(0) == place[2]
    for group in range(WIDTH // LANES):
        cols = slice(group * LANES, (group + 1) * LANES)
        for rows, source, f in ((key_rows, key_ref, 1), (value_rows, value_ref, 2)):
            spread(rows, source, cols, 2 * SUBS, step)
            rows[BASE - GAP - 2 : BASE - GAP, :] = edge_ref[f, :, lanes_of(block, group)].astype(jnp.float32)
        for lag in range(SHORT):
            taps[lag] = row(taps_ref[1, :, cols], lag) * KEEP_SCALE
            taps[SHORT + lag] = row(taps_ref[2, :, cols], lag)
        rates = rates_of(mix_ref[:, cols], tokens)
        fill(decays, jnp.exp(-rates))
        jumps = {d: jnp.exp(-rates * float(d * step)) for d in (1, 2, 4)}
        whole = jnp.exp(-rates * float(half))
        channel = place[1] + block * WIDTH + group * LANES + lane
        carried = None
        for part in range(2):
            base = BASE + part * SUBS * (step + GAP)
            first = counter[1] + place[0] + part * half + sub * step
            bits = counter[0] + first * jnp.int32(-1640531535) + channel * jnp.int32(-2048144777)

            def quad(j, carry):
                states, k1, k2, v1, v2, bits = carry
                values = []
                for u in range(QUAD):
                    k0 = across(key_rows, base + QUAD * j + u, step)
                    v0 = across(value_rows, base + QUAD * j + u, step)
                    keyed = taps[0] * k0 + taps[1] * k1 + taps[2] * k2
                    valued = taps[3] * v0 + taps[4] * v1 + taps[5] * v2
                    h = bits + jnp.int32(-1640531535) * u
                    h = h ^ lax.shift_right_logical(h, jnp.full_like(h, 16))
                    h = h * jnp.int32(2146121005)
                    h = h ^ lax.shift_right_logical(h, jnp.full_like(h, 15))
                    h = h * jnp.int32(-2073254261)
                    keep = (h & jnp.int32(-536870912)) != 0
                    values.append(jnp.where(keep, keyed * valued, 0.0))
                    k1, k2, v1, v2 = k0, k1, v0, v1
                wides = []
                for u in range(0, QUAD, 2):
                    rounded = jnp.concatenate(values[u : u + 2], axis=0).astype(jnp.bfloat16)
                    at = pl.multiple_of(part * half + (QUAD * j + u) * SUBS, 2 * SUBS)
                    gated_ref[block, pl.ds(at, 2 * SUBS), cols] = rounded
                    wide = rounded.astype(jnp.float32)
                    wides += [wide[:SUBS], wide[SUBS:]]
                after = []
                for r, x in enumerate(states):
                    a = decays[r]
                    for g in wides:
                        x = x * a + g
                    after.append(x)
                return (tuple(after), k1, k2, v1, v2, bits + jnp.int32((-1640531535 * QUAD + 2**31) % 2**32 - 2**31))

            zero = jnp.zeros((SUBS, LANES), jnp.float32)
            init = (
                (zero,) * ORDER,
                across(key_rows, base - GAP - 1, step),
                across(key_rows, base - GAP - 2, step),
                across(value_rows, base - GAP - 1, step),
                across(value_rows, base - GAP - 2, step),
                bits,
            )
            states = lax.fori_loop(0, step // QUAD, quad, init)[0]
            ends = []
            for r in range(ORDER):
                x = states[r]
                for d in (1, 2, 4):
                    x = x + row(jumps[d], r) * jnp.where(sub >= d, pltpu.roll(x, d, 0), 0.0)
                before = jnp.where(sub >= 1, pltpu.roll(x, 1, 0), 0.0)
                last = jnp.broadcast_to(x[SUBS - 1 : SUBS, :], (SUBS, LANES))
                if part == 1:
                    rate = row(rates, r)
                    before = before + jnp.exp(-rate * (sub * step).astype(jnp.float32)) * carried[r]
                    last = last + row(whole, r) * carried[r]
                start_ref[part, block, r, :, cols] = before
                ends.append(last)
            carried = ends
        end = jnp.concatenate([last[0:1, :] for last in carried], axis=0)

        @pl.when(is_mine)
        def _():
            mine_ref[:, cols] = end

        @pl.when(jnp.logical_not(is_mine))
        def _():
            other_ref[:, cols] = end


def query_setup(tokens, step, side_half, cols, lanes, query_ref, tail_ref, edge_ref, taps_ref, mix_ref, query_rows, decays, taps):
    spread(query_rows, query_ref, cols, SUBS, step)
    tail = tail_ref[tail_ref.shape[0] - SUBS :, cols].astype(jnp.float32)[SUBS - 2 :]
    edge = edge_ref[0, :, lanes].astype(jnp.float32)
    query_rows[BASE - GAP - 2 : BASE - GAP, :] = jnp.where(side_half == 0, edge, tail)
    for lag in range(SHORT):
        taps[lag] = row(taps_ref[0, :, cols], lag)
    rates = rates_of(mix_ref[:, cols], tokens)
    fill(decays, jnp.exp(-rates))
    return rates


def scan_quad(step, j, carry, gated_ref, block, base, cols, query_rows, decays, gains, taps, skip, emit):
    states, q1, q2 = carry
    values = []
    for u in range(0, QUAD, 2):
        at = pl.multiple_of(base + (QUAD * j + u) * SUBS, 2 * SUBS)
        wide = gated_ref[block, pl.ds(at, 2 * SUBS), cols].astype(jnp.float32)
        values += [wide[:SUBS], wide[SUBS:]]
    totals = [skip * g for g in values]
    after = []
    for r, x in enumerate(states):
        a = decays[r]
        c = gains[r]
        for u, g in enumerate(values):
            x = x * a + g
            totals[u] = totals[u] + x * c
        after.append(x)
    for u in range(QUAD):
        q0 = across(query_rows, BASE + QUAD * j + u, step)
        emit(u, taps[0] * q0 + taps[1] * q1 + taps[2] * q2, totals[u])
        q1, q2 = q0, q1
    return (tuple(after), q1, q2)


def gather(mixed_ref, mixed_rows, cols, step):
    for n in range(SUBS):
        at = n * (step + GAP)
        mixed_ref[n * step : (n + 1) * step, cols] = mixed_rows[at : at + step, :].astype(jnp.bfloat16)


def local_kernel(tokens, half, step, at, which, gated_ref, query_ref, tail_ref, edge_ref, taps_ref, mix_ref, residue_ref,
                 skip_ref, start_ref, *rest):
    local_ref, filtered_ref, query_rows, decays, gains, taps = rest[-6:]
    block = at + pl.program_id(0)
    base = which[0] * half
    for group in range(WIDTH // LANES):
        cols = slice(group * LANES, (group + 1) * LANES)
        lanes = lanes_of(block, group)
        query_setup(tokens, step, which[0], cols, lanes, query_ref, tail_ref, edge_ref, taps_ref, mix_ref, query_rows, decays, taps)
        fill(gains, residue_ref[:, cols])
        skip = row(skip_ref[:, cols], 0)

        def quad(j, carry):
            def emit(u, query, total):
                spot = pl.ds(pl.multiple_of((QUAD * j + u) * SUBS, SUBS), SUBS)
                local_ref[block, spot, cols] = total
                filtered_ref[block, spot, cols] = query

            return scan_quad(step, j, carry, gated_ref, block, base, cols, query_rows, decays, gains, taps, skip, emit)

        states = tuple(start_ref[which[0], block, r, :, cols] for r in range(ORDER))
        q1, q2 = across(query_rows, BASE - GAP - 1, step), across(query_rows, BASE - GAP - 2, step)
        lax.fori_loop(0, step // QUAD, quad, (states, q1, q2))


def blend_kernel(tokens, half, step, which, gated_ref, query_ref, tail_ref, edge_ref, taps_ref, mix_ref, residue_ref,
                 skip_ref, start_ref, own_ref, got_ref, mixed_ref, query_rows, decays, gains, taps, mixed_rows):
    sub = lax.broadcasted_iota(jnp.int32, (SUBS, LANES), 0)
    block = pl.program_id(0)
    base = which[0] * half
    offset = (base + sub * step).astype(jnp.float32)
    for group in range(WIDTH // LANES):
        cols = slice(group * LANES, (group + 1) * LANES)
        lanes = lanes_of(pl.program_id(0), group)
        rates = query_setup(tokens, step, which[0], cols, lanes, query_ref, tail_ref, edge_ref, taps_ref, mix_ref, query_rows, decays, taps)
        fill(gains, residue_ref[:, cols])
        skip = row(skip_ref[:, cols], 0)
        into = state_of(own_ref, got_ref, which[1], group)

        def quad(j, carry):
            def emit(u, query, total):
                mixed_rows[pl.ds(QUAD * j + u, SUBS, stride=step + GAP), :] = query * total

            return scan_quad(step, j, carry, gated_ref, block, base, cols, query_rows, decays, gains, taps, skip, emit)

        states = tuple(
            start_ref[which[0], block, r, :, cols] + jnp.exp(-row(rates, r) * offset) * row(into, r) for r in range(ORDER)
        )
        q1, q2 = across(query_rows, BASE - GAP - 1, step), across(query_rows, BASE - GAP - 2, step)
        lax.fori_loop(0, step // QUAD, quad, (states, q1, q2))
        gather(mixed_ref, mixed_rows, cols, step)


def carry_kernel(tokens, half, step, which, local_ref, filtered_ref, mix_ref, residue_ref, own_ref, got_ref,
                 mixed_ref, decays, mixed_rows):
    sub = lax.broadcasted_iota(jnp.int32, (SUBS, LANES), 0)
    block = pl.program_id(0)
    offset = (which[0] * half + sub * step + 1).astype(jnp.float32)
    for group in range(WIDTH // LANES):
        cols = slice(group * LANES, (group + 1) * LANES)
        rates = rates_of(mix_ref[:, cols], tokens)
        fill(decays, jnp.exp(-rates))
        into = state_of(own_ref, got_ref, which[1], group) * residue_ref[:, cols]

        def quad(j, states):
            totals = [None] * QUAD
            after = []
            for r, x in enumerate(states):
                a = decays[r]
                for u in range(QUAD):
                    totals[u] = x if totals[u] is None else totals[u] + x
                    x = x * a
                after.append(x)
            for u in range(QUAD):
                at = pl.multiple_of((QUAD * j + u) * SUBS, SUBS)
                spot = pl.ds(at, SUBS)
                value = filtered_ref[block, spot, cols] * (local_ref[block, spot, cols] + totals[u])
                mixed_rows[pl.ds(QUAD * j + u, SUBS, stride=step + GAP), :] = value
            return tuple(after)

        states = tuple(jnp.exp(-row(rates, r) * offset) * row(into, r) for r in range(ORDER))
        lax.fori_loop(0, step // QUAD, quad, states)
        gather(mixed_ref, mixed_rows, cols, step)


def project_kernel(mixed_ref, weight_ref, out_ref):
    out_ref[...] = jnp.dot(mixed_ref[...], weight_ref[...], preferred_element_type=jnp.float32).astype(out_ref.dtype)


def combine_kernel(own_ref, got_ref, *rest):
    rest[-1][...] = (own_ref[...] + got_ref[...].astype(jnp.float32)).astype(jnp.bfloat16)


def table(count=ORDER):
    return pltpu.VMEM((count, SUBS, LANES), jnp.float32)


def room(mib):
    return pltpu.CompilerParams(vmem_limit_bytes=mib * 2**20)


def cost(vectors, moved):
    return pl.CostEstimate(flops=vectors, bytes_accessed=moved, transcendentals=0)


def gate(counter, place, planes, edge, taps, mix, tokens):
    rows, channels = planes.shape[1:]
    half = rows // 2
    step = half // SUBS
    blocks = channels // WIDTH
    spread_rows = BASE + 2 * SUBS * (step + GAP)
    first = lambda b, owner: jnp.clip(b - owner * (blocks // 2), 0, blocks // 2 - 1)
    return pl.pallas_call(
        lambda *refs: gate_kernel(tokens, half, step, *refs),
        out_shape=(
            pltpu.VMEM((blocks, rows, WIDTH), jnp.bfloat16),
            pltpu.VMEM((2, blocks, ORDER, SUBS, WIDTH), jnp.float32),
            jax.ShapeDtypeStruct((ORDER, channels // 2), jnp.float32),
            jax.ShapeDtypeStruct((ORDER, channels // 2), jnp.float32),
        ),
        grid_spec=pltpu.PrefetchScalarGridSpec(
            num_scalar_prefetch=2,
            grid=(blocks,),
            in_specs=[
                pl.BlockSpec((None, rows, WIDTH), lambda b, c, s: (1, 0, b)),
                pl.BlockSpec((None, rows, WIDTH), lambda b, c, s: (2, 0, b)),
                pl.BlockSpec(memory_space=pltpu.VMEM),
                pl.BlockSpec((3, SHORT, WIDTH), lambda b, c, s: (0, 0, b)),
                pl.BlockSpec((ORDER, WIDTH), lambda b, c, s: (0, b)),
            ],
            out_specs=(
                pl.BlockSpec(memory_space=pltpu.VMEM),
                pl.BlockSpec(memory_space=pltpu.VMEM),
                pl.BlockSpec((ORDER, WIDTH), lambda b, c, s: (0, first(b, s[2]))),
                pl.BlockSpec((ORDER, WIDTH), lambda b, c, s: (0, first(b, 1 - s[2]))),
            ),
            scratch_shapes=[pltpu.VMEM((spread_rows, LANES), jnp.float32)] * 2 + [table(), table(2 * SHORT)],
        ),
        name="gate",
        compiler_params=room(16),
        cost_estimate=cost(15 * 10**9, 4 * rows * channels),
    )(counter, place, planes, planes, edge, taps, mix)


def scan_specs(half, at):
    tail = half // 16 - 1
    return [
        pl.BlockSpec(memory_space=pltpu.VMEM),
        pl.BlockSpec((None, half, WIDTH), lambda b, s: (0, s[0], at + b)),
        pl.BlockSpec((None, 16, WIDTH), lambda b, s: (0, tail, at + b)),
        pl.BlockSpec(memory_space=pltpu.VMEM),
        pl.BlockSpec((3, SHORT, WIDTH), lambda b, s: (0, 0, at + b)),
        pl.BlockSpec((ORDER, WIDTH), lambda b, s: (0, at + b)),
        pl.BlockSpec((ORDER, WIDTH), lambda b, s: (0, at + b)),
        pl.BlockSpec((1, WIDTH), lambda b, s: (0, at + b)),
        pl.BlockSpec(memory_space=pltpu.VMEM),
    ]


def scan_scratch(step):
    return [pltpu.VMEM((BASE + SUBS * (step + GAP), LANES), jnp.float32), table(), table(), table(SHORT)]


def local(which, operands, tokens, piece, pieces, before):
    blocks, rows = operands[0].shape[:2]
    half = rows // 2
    step = half // SUBS
    shape = pltpu.VMEM((blocks, half, WIDTH), jnp.float32)
    blocks = blocks // pieces
    at = piece * blocks
    out = pl.BlockSpec(memory_space=pltpu.VMEM)
    return pl.pallas_call(
        lambda *refs: local_kernel(tokens, half, step, at, *refs),
        out_shape=(shape, shape),
        grid_spec=pltpu.PrefetchScalarGridSpec(
            num_scalar_prefetch=1,
            grid=(blocks,),
            in_specs=scan_specs(half, at) + [pl.BlockSpec(memory_space=pltpu.VMEM)] * len(before),
            out_specs=(out, out),
            scratch_shapes=scan_scratch(step),
        ),
        input_output_aliases={1 + len(operands) + k: k for k in range(len(before))},
        name="local",
        compiler_params=room(16),
        cost_estimate=cost(10**10 // pieces, half * blocks * WIDTH),
    )(which, *operands, *before)


def carry(which, parts, mix, residue, own, got, tokens):
    blocks, half = parts[0].shape[:2]
    channels = blocks * WIDTH
    step = half // SUBS
    block = pl.BlockSpec((half, WIDTH), lambda b, s: (0, b))
    mode = pl.BlockSpec((ORDER, WIDTH), lambda b, s: (0, b))
    return pl.pallas_call(
        lambda *refs: carry_kernel(tokens, half, step, *refs),
        out_shape=jax.ShapeDtypeStruct((half, channels), jnp.bfloat16),
        grid_spec=pltpu.PrefetchScalarGridSpec(
            num_scalar_prefetch=1,
            grid=(blocks,),
            in_specs=[pl.BlockSpec(memory_space=pltpu.VMEM)] * 2 + [mode, mode] + [pl.BlockSpec(memory_space=pltpu.VMEM)] * 2,
            out_specs=block,
            scratch_shapes=[table(), pltpu.VMEM((SUBS * (step + GAP), LANES), jnp.float32)],
        ),
        name="carry",
        compiler_params=room(16),
        cost_estimate=cost(5 * 10**9, half * channels),
    )(which, *parts, mix, residue, own, got)


def blend(which, operands, own, got, tokens):
    blocks, rows = operands[0].shape[:2]
    channels = blocks * WIDTH
    half = rows // 2
    step = half // SUBS
    return pl.pallas_call(
        lambda *refs: blend_kernel(tokens, half, step, *refs),
        out_shape=jax.ShapeDtypeStruct((half, channels), jnp.bfloat16),
        grid_spec=pltpu.PrefetchScalarGridSpec(
            num_scalar_prefetch=1,
            grid=(blocks,),
            in_specs=scan_specs(half, 0) + [pl.BlockSpec(memory_space=pltpu.VMEM)] * 2,
            out_specs=pl.BlockSpec((half, WIDTH), lambda b, s: (0, b)),
            scratch_shapes=scan_scratch(step) + [pltpu.VMEM((SUBS * (step + GAP), LANES), jnp.float32)],
        ),
        name="blend",
        compiler_params=room(16),
        cost_estimate=cost(9 * 10**9, 2 * half * channels),
    )(which, *operands, own, got)


def project(mixed, weight, first, cols, dtype):
    rows, depth = mixed.shape
    at = first // TILE_COLS
    return pl.pallas_call(
        project_kernel,
        out_shape=jax.ShapeDtypeStruct((rows, cols), dtype),
        grid=(cols // TILE_COLS,),
        in_specs=[
            pl.BlockSpec((rows, depth), lambda n: (0, 0)),
            pl.BlockSpec((depth, TILE_COLS), lambda n: (0, at + n)),
        ],
        out_specs=pl.BlockSpec((rows, TILE_COLS), lambda n: (0, n)),
        compiler_params=room(16),
        cost_estimate=cost(2 * rows * depth * cols, 2 * (rows * depth + depth * cols)),
    )(mixed, weight)


def combine(own, got, first, before):
    rows, cols = got.shape
    at = first // cols
    block = pl.BlockSpec((rows, cols), lambda n: (0, at))
    return pl.pallas_call(
        combine_kernel,
        out_shape=jax.ShapeDtypeStruct(own.shape, jnp.bfloat16),
        grid=(1,),
        in_specs=[block, pl.BlockSpec(memory_space=pltpu.VMEM)]
        + [pl.BlockSpec(memory_space=pl.ANY)] * len(before),
        out_specs=block,
        input_output_aliases={2: 0} if before else {},
        name="combine",
        compiler_params=room(8),
        cost_estimate=cost(rows * cols, 8 * rows * cols),
    )(own, got, *before)


def states_before(mine, other, mix, tokens, rows, index, count, between):
    core = index % 2
    width = mine.shape[1]
    rates = rates_of(lax.dynamic_slice_in_dim(mix, core * width, width, 1), tokens)
    decay = lambda chunks: jnp.exp(-rates * float(rows * chunks))
    steps = [decay(n) for n in (1, 2, 4)]
    assert count == 16

    def ring(value, pairs):
        return lax.ppermute(value, "ctx", pairs)

    sibling = ring(other, [(i, i ^ 1) for i in range(count)])
    early = jnp.where(core == 0, mine, sibling)
    late = jnp.where(core == 0, sibling, mine)
    chip = steps[0] * early + late
    beside = ring(chip, [(i, i ^ 2) for i in range(count)])
    between(0)
    between(1)
    upper = (index // 2) % 2 == 1
    group = jnp.where(upper, steps[1] * beside + chip, steps[1] * chip + beside)
    ring_at = index // 4
    odd = ring_at % 2 == 1
    near = ring(group, [(i, i ^ 4) for i in range(count)])
    between(2)
    couple = jnp.where(odd, steps[2] * near + group, steps[2] * group + near)
    far = ring(couple, [(i, (3 - i // 4) * 4 + i % 4) for i in range(count)])
    between(3)
    state = jnp.where(ring_at >= 2, jnp.where(odd, steps[2] * far, far), 0.0) + jnp.where(odd, near, 0.0)
    state = jnp.where(upper, steps[1] * state + beside, state)
    following = steps[0] * state + early
    own = jnp.where(core == 0, state, following)
    sent = jnp.where(core == 0, following, state)
    return own, ring(sent, [(i, i ^ 1) for i in range(count)])


def body(features, short_filter, mode_residue, decay_mix, skip_gain, counter, out_weight):
    rows = features.shape[0]
    channels = features.shape[2]
    count = lax.axis_size("ctx")
    tokens = rows * count
    index = lax.axis_index("ctx")
    side = lax.axis_index("ch")
    planes = jnp.transpose(features, (1, 0, 2))
    far_memory = lambda x: pltpu.with_memory_space_constraint(x, pltpu.HBM)
    edge = lax.ppermute(planes[:, rows - (SHORT - 1) :], "ctx", [(i, i + 1) for i in range(count - 1)])
    slot = jnp.arange(4, dtype=jnp.int32)

    def scalars(*values):
        out = jnp.zeros((4,), jnp.int32)
        for k, value in enumerate(values):
            out = jnp.where(slot == k, value, out)
        return out

    place = scalars(index * rows, side * channels, index % 2)
    to_send = scalars(1 - side, index % 2)
    to_keep = scalars(side, index % 2)
    planes, taps, mix, residue, skip = map(far_memory, (planes, short_filter, decay_mix, mode_residue, skip_gain[None]))
    gated, start, mine, other = gate(counter, place, planes, edge, taps, mix, tokens)
    operands = (gated, planes, planes, edge, taps, mix, residue, skip, start)
    parts = [()]

    def between(piece):
        parts[0] = local(to_send, operands, tokens, piece, 4, parts[0])

    own, got = states_before(mine, other, decay_mix, tokens, rows, index, count, between)
    sent = carry(to_send, parts[0], mix, residue, own, got, tokens)
    outs = out_weight.shape[1]
    received = []
    for first in range(0, outs, SEND_COLS):
        part = project(sent, out_weight, first, SEND_COLS, jnp.bfloat16)
        received.append(lax.ppermute(part, "ch", [(0, 1), (1, 0)]))
    own, part = lax.optimization_barrier((own, part))
    kept = blend(to_keep, operands, own, got, tokens)
    total = project(kept, out_weight, 0, outs, jnp.float32)
    done = ()
    for k, first in enumerate(range(0, outs, SEND_COLS)):
        done = (combine(total, received[k], first, done),)
    return done[0]


def solution(mesh):
    placed = (
        P(("dp", "ctx"), None, "ch"),
        P(None, None, "ch"),
        P(None, "ch"),
        P(None, "ch"),
        P("ch"),
        P("dp"),
        P("ch", None),
    )

    return jax.shard_map(body, mesh=mesh, in_specs=placed, out_specs=P(("dp", "ctx", "ch"), None), check_vma=False)
```

```python
import math

import jax
import jax.numpy as jnp
from jax import lax
from jax.experimental import pallas as pl
from jax.experimental.pallas import tpu as pltpu
from jax.sharding import PartitionSpec as P


SHORT = 3
ORDER = 16
LANES = 128
SUBS = 8
WIDTH = 2 * LANES
KEEP_SCALE = 8.0 / 7.0
TILE_COLS = 256
BASE = 40
GAP = 4
QUAD = 4
GATE_STEPS = 8


def rates_of(mix, length):
    return jnp.exp(-((1.0 - mix) * math.log(length) + mix * math.log(30.0)))


def row(table, index):
    return jnp.broadcast_to(table[index : index + 1, :], (SUBS, table.shape[1]))


def spread(rows, source, first, cols, count, step):
    for n in range(count):
        at = BASE + n * (step + GAP)
        spot = pl.ds(pl.multiple_of(first + n * step, step), step)
        rows[at : at + step, :] = source[spot, cols].astype(jnp.float32)


def across(rows, at, step):
    return rows[pl.ds(at, SUBS, stride=step + GAP), :]


def chunks_of(outs):
    sizes = [TILE_COLS] + [2 * TILE_COLS] * ((outs - TILE_COLS) // (2 * TILE_COLS))
    sizes += [TILE_COLS] * ((outs - sum(sizes)) // TILE_COLS)
    return [(sum(sizes[:k]), size) for k, size in enumerate(sizes)]


def lanes_of(group):
    return pl.ds(pl.multiple_of(group * LANES, LANES), LANES)


def state_of(own_ref, got_ref, core, group, groups):
    lanes = lanes_of(group % (groups // 2))
    return jnp.where(group // (groups // 2) == core, own_ref[:, lanes], got_ref[:, lanes])


def fill(table, values):
    for r in range(ORDER):
        table[r] = row(values, r)


def gate_kernel(tokens, half, step, counter, place, key_ref, value_ref, edge_ref, taps_ref, mix_ref,
                gated_ref, start_ref, mine_ref, other_ref, key_rows, value_rows, decays, taps):
    block = pl.program_id(0)
    lane = lax.broadcasted_iota(jnp.int32, (SUBS, LANES), 1)
    sub = lax.broadcasted_iota(jnp.int32, (SUBS, LANES), 0)
    is_mine = (block * 2) // pl.num_programs(0) == place[2]
    for group in range(WIDTH // LANES):
        cols = slice(group * LANES, (group + 1) * LANES)
        place_of = block * (WIDTH // LANES) + group
        for rows, source, f in ((key_rows, key_ref, 1), (value_rows, value_ref, 2)):
            spread(rows, source, 0, cols, 2 * SUBS, step)
            rows[BASE - GAP - 2 : BASE - GAP, :] = edge_ref[f, :, lanes_of(place_of)].astype(jnp.float32)
        for lag in range(SHORT):
            taps[lag] = row(taps_ref[1, :, cols], lag) * KEEP_SCALE
            taps[SHORT + lag] = row(taps_ref[2, :, cols], lag)
        rates = rates_of(mix_ref[:, cols], tokens)
        fill(decays, jnp.exp(-rates))
        jumps = {d: jnp.exp(-rates * float(d * step)) for d in (1, 2, 4)}
        whole = jnp.exp(-rates * float(half))
        channel = place[1] + block * WIDTH + group * LANES + lane
        carried = None
        for part in range(2):
            base = BASE + part * SUBS * (step + GAP)
            first = counter[1] + place[0] + part * half + sub * step
            bits = counter[0] + first * jnp.int32(-1640531535) + channel * jnp.int32(-2048144777)

            def quad(j, carry):
                states, k1, k2, v1, v2, bits = carry
                values = []
                for u in range(GATE_STEPS):
                    k0 = across(key_rows, base + GATE_STEPS * j + u, step)
                    v0 = across(value_rows, base + GATE_STEPS * j + u, step)
                    keyed = taps[0] * k0 + taps[1] * k1 + taps[2] * k2
                    valued = taps[3] * v0 + taps[4] * v1 + taps[5] * v2
                    h = bits + jnp.int32(-1640531535) * u
                    h = h ^ lax.shift_right_logical(h, jnp.full_like(h, 16))
                    h = h * jnp.int32(2146121005)
                    h = h ^ lax.shift_right_logical(h, jnp.full_like(h, 15))
                    h = h * jnp.int32(-2073254261)
                    keep = (h & jnp.int32(-536870912)) != 0
                    values.append(jnp.where(keep, keyed * valued, 0.0))
                    k1, k2, v1, v2 = k0, k1, v0, v1
                wides = []
                for u in range(0, GATE_STEPS, 2):
                    rounded = jnp.concatenate(values[u : u + 2], axis=0).astype(jnp.bfloat16)
                    at = pl.multiple_of(part * half + (GATE_STEPS * j + u) * SUBS, 2 * SUBS)
                    gated_ref[place_of, pl.ds(at, 2 * SUBS), :] = rounded
                    wide = rounded.astype(jnp.float32)
                    wides += [wide[:SUBS], wide[SUBS:]]
                after = []
                for r, x in enumerate(states):
                    a = decays[r]
                    for g in wides:
                        x = x * a + g
                    after.append(x)
                return (tuple(after), k1, k2, v1, v2, bits + jnp.int32((-1640531535 * GATE_STEPS + 2**31) % 2**32 - 2**31))

            zero = jnp.zeros((SUBS, LANES), jnp.float32)
            init = (
                (zero,) * ORDER,
                across(key_rows, base - GAP - 1, step),
                across(key_rows, base - GAP - 2, step),
                across(value_rows, base - GAP - 1, step),
                across(value_rows, base - GAP - 2, step),
                bits,
            )
            states = lax.fori_loop(0, step // GATE_STEPS, quad, init)[0]
            ends = []
            for r in range(ORDER):
                x = states[r]
                for d in (1, 2, 4):
                    x = x + row(jumps[d], r) * jnp.where(sub >= d, pltpu.roll(x, d, 0), 0.0)
                before = jnp.where(sub >= 1, pltpu.roll(x, 1, 0), 0.0)
                last = jnp.broadcast_to(x[SUBS - 1 : SUBS, :], (SUBS, LANES))
                if part == 1:
                    rate = row(rates, r)
                    before = before + jnp.exp(-rate * (sub * step).astype(jnp.float32)) * carried[r]
                    last = last + row(whole, r) * carried[r]
                start_ref[part, place_of, r] = before
                ends.append(last)
            carried = ends
        end = jnp.concatenate([last[0:1, :] for last in carried], axis=0)

        @pl.when(is_mine)
        def _():
            mine_ref[:, cols] = end

        @pl.when(jnp.logical_not(is_mine))
        def _():
            other_ref[:, cols] = end


def query_setup(tokens, half, step, which, lanes, planes_ref, edge_ref, taps_ref, mix_ref, query_rows, decays, taps):
    spread(query_rows, planes_ref.at[0], which * half, lanes, SUBS, step)
    tail = planes_ref[0, half - 2 * SUBS : half, lanes].astype(jnp.float32)[2 * SUBS - 2 :]
    edge = edge_ref[0, :, lanes].astype(jnp.float32)
    query_rows[BASE - GAP - 2 : BASE - GAP, :] = jnp.where(which == 0, edge, tail)
    for lag in range(SHORT):
        taps[lag] = row(taps_ref[0, :, lanes], lag)
    rates = rates_of(mix_ref[:, lanes], tokens)
    fill(decays, jnp.exp(-rates))
    return rates


def scan_quad(step, j, carry, gated_ref, base, query_rows, decays, gains, taps, skip, emit):
    states, q1, q2 = carry
    values = []
    for u in range(0, QUAD, 2):
        at = pl.multiple_of(base + (QUAD * j + u) * SUBS, 2 * SUBS)
        wide = gated_ref[pl.ds(at, 2 * SUBS), :].astype(jnp.float32)
        values += [wide[:SUBS], wide[SUBS:]]
    totals = [skip * g for g in values]
    after = []
    for r, x in enumerate(states):
        a = decays[r]
        c = gains[r]
        for u, g in enumerate(values):
            x = x * a + g
            totals[u] = totals[u] + x * c
        after.append(x)
    for u in range(QUAD):
        q0 = across(query_rows, BASE + QUAD * j + u, step)
        emit(u, taps[0] * q0 + taps[1] * q1 + taps[2] * q2, totals[u])
        q1, q2 = q0, q1
    return (tuple(after), q1, q2)


def gather(mixed_ref, mixed_rows, lanes, step):
    for n in range(SUBS):
        at = n * (step + GAP)
        mixed_ref[n * step : (n + 1) * step, lanes] = mixed_rows[at : at + step, :].astype(jnp.bfloat16)


def local_kernel(tokens, half, step, first, last, which, gated_ref, planes_ref, edge_ref, taps_ref, mix_ref,
                 residue_ref, skip_ref, start_ref, *rest):
    local_ref, filtered_ref, query_rows, decays, gains, taps = rest[-6:]

    @pl.loop(first, last)
    def _(group):
        lanes = lanes_of(group)
        query_setup(tokens, half, step, which[0], lanes, planes_ref, edge_ref, taps_ref, mix_ref, query_rows, decays, taps)
        fill(gains, residue_ref[:, lanes])
        skip = row(skip_ref[:, lanes], 0)

        def quad(j, carry):
            def emit(u, query, total):
                spot = pl.ds(pl.multiple_of((QUAD * j + u) * SUBS, SUBS), SUBS)
                local_ref[group, spot, :] = total
                filtered_ref[group, spot, :] = query

            return scan_quad(step, j, carry, gated_ref.at[group], which[0] * half, query_rows, decays, gains, taps, skip, emit)

        states = tuple(start_ref[which[0], group, r] for r in range(ORDER))
        q1, q2 = across(query_rows, BASE - GAP - 1, step), across(query_rows, BASE - GAP - 2, step)
        lax.fori_loop(0, step // QUAD, quad, (states, q1, q2))


def blend_kernel(tokens, half, step, groups, which, gated_ref, planes_ref, edge_ref, taps_ref, mix_ref, residue_ref,
                 skip_ref, start_ref, own_ref, got_ref, mixed_ref, query_rows, decays, gains, taps, mixed_rows):
    sub = lax.broadcasted_iota(jnp.int32, (SUBS, LANES), 0)
    offset = (which[0] * half + sub * step).astype(jnp.float32)

    @pl.loop(0, groups)
    def _(group):
        lanes = lanes_of(group)
        rates = query_setup(tokens, half, step, which[0], lanes, planes_ref, edge_ref, taps_ref, mix_ref, query_rows, decays, taps)
        fill(gains, residue_ref[:, lanes])
        skip = row(skip_ref[:, lanes], 0)
        into = state_of(own_ref, got_ref, which[1], group, groups)

        def quad(j, carry):
            def emit(u, query, total):
                mixed_rows[pl.ds(QUAD * j + u, SUBS, stride=step + GAP), :] = query * total

            return scan_quad(step, j, carry, gated_ref.at[group], which[0] * half, query_rows, decays, gains, taps, skip, emit)

        states = tuple(
            start_ref[which[0], group, r] + jnp.exp(-row(rates, r) * offset) * row(into, r) for r in range(ORDER)
        )
        q1, q2 = across(query_rows, BASE - GAP - 1, step), across(query_rows, BASE - GAP - 2, step)
        lax.fori_loop(0, step // QUAD, quad, (states, q1, q2))
        gather(mixed_ref, mixed_rows, lanes, step)


def carry_kernel(tokens, half, step, groups, mine, which, local_ref, filtered_ref, mix_ref, residue_ref, state_ref, *rest):
    mixed_ref, decays, mixed_rows = rest[-3:]
    sub = lax.broadcasted_iota(jnp.int32, (SUBS, LANES), 0)
    offset = (which[0] * half + sub * step + 1).astype(jnp.float32)

    base = (which[1] if mine else 1 - which[1]) * groups

    @pl.loop(0, groups)
    def _(at):
        group = base + at
        lanes = lanes_of(group)
        rates = rates_of(mix_ref[:, lanes], tokens)
        fill(decays, jnp.exp(-rates))
        into = state_ref[:, lanes_of(at)] * residue_ref[:, lanes]

        def quad(j, states):
            totals = [None] * QUAD
            after = []
            for r, x in enumerate(states):
                a = decays[r]
                for u in range(QUAD):
                    totals[u] = x if totals[u] is None else totals[u] + x
                    x = x * a
                after.append(x)
            for u in range(QUAD):
                spot = pl.ds(pl.multiple_of((QUAD * j + u) * SUBS, SUBS), SUBS)
                value = filtered_ref[group, spot, :] * (local_ref[group, spot, :] + totals[u])
                mixed_rows[pl.ds(QUAD * j + u, SUBS, stride=step + GAP), :] = value
            return tuple(after)

        states = tuple(jnp.exp(-row(rates, r) * offset) * row(into, r) for r in range(ORDER))
        lax.fori_loop(0, step // QUAD, quad, states)
        gather(mixed_ref, mixed_rows, lanes, step)


def project_kernel(mixed_ref, weight_ref, out_ref):
    out_ref[...] = jnp.dot(mixed_ref[...], weight_ref[...], preferred_element_type=jnp.float32).astype(out_ref.dtype)


def combine_kernel(own_ref, got_ref, *rest):
    lanes = pl.ds(pl.multiple_of(pl.program_id(0) * TILE_COLS, TILE_COLS), TILE_COLS)
    rest[-1][...] = (own_ref[...] + got_ref[:, lanes].astype(jnp.float32)).astype(jnp.bfloat16)


def table(count=ORDER):
    return pltpu.VMEM((count, SUBS, LANES), jnp.float32)


def room(mib):
    return pltpu.CompilerParams(vmem_limit_bytes=mib * 2**20)


def cost(vectors, moved):
    return pl.CostEstimate(flops=vectors, bytes_accessed=moved, transcendentals=0)


def gate(counter, place, planes, edge, taps, mix, tokens):
    rows, channels = planes.shape[1:]
    half = rows // 2
    step = half // SUBS
    blocks = channels // WIDTH
    spread_rows = BASE + 2 * SUBS * (step + GAP)
    first = lambda b, owner: jnp.clip(b - owner * (blocks // 2), 0, blocks // 2 - 1)
    return pl.pallas_call(
        lambda *refs: gate_kernel(tokens, half, step, *refs),
        out_shape=(
            pltpu.VMEM((channels // LANES, rows, LANES), jnp.bfloat16),
            pltpu.VMEM((2, channels // LANES, ORDER, SUBS, LANES), jnp.float32),
            jax.ShapeDtypeStruct((ORDER, channels // 2), jnp.float32),
            jax.ShapeDtypeStruct((ORDER, channels // 2), jnp.float32),
        ),
        grid_spec=pltpu.PrefetchScalarGridSpec(
            num_scalar_prefetch=2,
            grid=(blocks,),
            in_specs=[
                pl.BlockSpec((None, rows, WIDTH), lambda b, c, s: (1, 0, b)),
                pl.BlockSpec((None, rows, WIDTH), lambda b, c, s: (2, 0, b)),
                pl.BlockSpec(memory_space=pltpu.VMEM),
                pl.BlockSpec((3, SHORT, WIDTH), lambda b, c, s: (0, 0, b)),
                pl.BlockSpec((ORDER, WIDTH), lambda b, c, s: (0, b)),
            ],
            out_specs=(
                pl.BlockSpec(memory_space=pltpu.VMEM),
                pl.BlockSpec(memory_space=pltpu.VMEM),
                pl.BlockSpec((ORDER, WIDTH), lambda b, c, s: (0, first(b, s[2]))),
                pl.BlockSpec((ORDER, WIDTH), lambda b, c, s: (0, first(b, 1 - s[2]))),
            ),
            scratch_shapes=[pltpu.VMEM((spread_rows, LANES), jnp.float32)] * 2 + [table(), table(2 * SHORT)],
        ),
        name="gate",
        compiler_params=room(16),
        cost_estimate=cost(15 * 10**9, 4 * rows * channels),
    )(counter, place, planes, planes, edge, taps, mix)


def scan_scratch(step):
    return [pltpu.VMEM((BASE + SUBS * (step + GAP), LANES), jnp.float32), table(), table(), table(SHORT)]


def resident(kernel, which, operands, out_shape, scratch, aliases, time):
    several = isinstance(out_shape, tuple)
    place = pl.BlockSpec(memory_space=pltpu.VMEM)
    return pl.pallas_call(
        kernel,
        out_shape=out_shape,
        grid_spec=pltpu.PrefetchScalarGridSpec(
            num_scalar_prefetch=1,
            grid=(1,),
            in_specs=[place] * len(operands),
            out_specs=(place,) * len(out_shape) if several else place,
            scratch_shapes=scratch,
        ),
        input_output_aliases=aliases,
        compiler_params=room(16),
        cost_estimate=cost(int(time * 10**9), 2**20),
    )(which, *operands)


def local(which, operands, tokens, first, last, before):
    groups, rows = operands[0].shape[:2]
    half = rows // 2
    step = half // SUBS
    shape = pltpu.VMEM((groups, half, LANES), jnp.float32)
    first, last = first * groups // 4, last * groups // 4
    return resident(
        lambda *refs: local_kernel(tokens, half, step, first, last, *refs), which, (*operands, *before), (shape, shape),
        scan_scratch(step), {1 + len(operands) + k: k for k in range(len(before))}, 0.55 * (last - first),
    )


def carry(which, parts, mix, residue, state, mine, before, tokens):
    groups, half = parts[0].shape[:2]
    step = half // SUBS
    return resident(
        lambda *refs: carry_kernel(tokens, half, step, groups // 2, mine, *refs), which,
        (*parts, mix, residue, state, *before), pltpu.VMEM((half, groups * LANES), jnp.bfloat16),
        [table(), pltpu.VMEM((SUBS * (step + GAP), LANES), jnp.float32)], {6: 0} if before else {}, 2.5,
    )


def blend(which, operands, own, got, tokens):
    groups, rows = operands[0].shape[:2]
    half = rows // 2
    step = half // SUBS
    return resident(
        lambda *refs: blend_kernel(tokens, half, step, groups, *refs), which, (*operands, own, got),
        jax.ShapeDtypeStruct((half, groups * LANES), jnp.bfloat16),
        scan_scratch(step) + [pltpu.VMEM((SUBS * (step + GAP), LANES), jnp.float32)], {}, 9,
    )


def project(mixed, weight, first, cols, dtype):
    rows, depth = mixed.shape
    at = first // TILE_COLS
    return pl.pallas_call(
        project_kernel,
        out_shape=jax.ShapeDtypeStruct((rows, cols), dtype),
        grid=(cols // TILE_COLS,),
        in_specs=[
            pl.BlockSpec((rows, depth), lambda n: (0, 0)),
            pl.BlockSpec((depth, TILE_COLS), lambda n: (0, at + n)),
        ],
        out_specs=pl.BlockSpec((rows, TILE_COLS), lambda n: (0, n)),
        compiler_params=room(16),
        cost_estimate=cost(2 * rows * depth * cols, 2 * (rows * depth + depth * cols)),
    )(mixed, weight)


def combine(own, got, first, before):
    rows, cols = got.shape
    at = first // TILE_COLS
    block = pl.BlockSpec((rows, TILE_COLS), lambda n: (0, at + n))
    return pl.pallas_call(
        combine_kernel,
        out_shape=jax.ShapeDtypeStruct(own.shape, jnp.bfloat16),
        grid=(cols // TILE_COLS,),
        in_specs=[block, pl.BlockSpec(memory_space=pltpu.VMEM)]
        + [pl.BlockSpec(memory_space=pl.ANY)] * len(before),
        out_specs=block,
        input_output_aliases={2: 0} if before else {},
        name="combine",
        compiler_params=room(8),
        cost_estimate=cost(rows * cols, 8 * rows * cols),
    )(own, got, *before)


def states_before(mine, other, mix, tokens, rows, index, count, between):
    core = index % 2
    width = mine.shape[1]
    rates = rates_of(lax.dynamic_slice_in_dim(mix, core * width, width, 1), tokens)
    decay = lambda chunks: jnp.exp(-rates * float(rows * chunks))
    steps = [decay(n) for n in (1, 2, 4)]
    assert count == 16

    def ring(value, pairs):
        return lax.ppermute(value, "ctx", pairs)

    sibling = ring(other, [(i, i ^ 1) for i in range(count)])
    early = jnp.where(core == 0, mine, sibling)
    late = jnp.where(core == 0, sibling, mine)
    chip = steps[0] * early + late
    beside = ring(chip, [(i, i ^ 2) for i in range(count)])
    between(0)
    upper = (index // 2) % 2 == 1
    group = jnp.where(upper, steps[1] * beside + chip, steps[1] * chip + beside)
    ring_at = index // 4
    odd = ring_at % 2 == 1
    near = ring(group, [(i, i ^ 4) for i in range(count)])
    between(1)
    couple = jnp.where(odd, steps[2] * near + group, steps[2] * group + near)
    far = ring(couple, [(i, (3 - i // 4) * 4 + i % 4) for i in range(count)])
    between(2)
    state = jnp.where(ring_at >= 2, jnp.where(odd, steps[2] * far, far), 0.0) + jnp.where(odd, near, 0.0)
    state = jnp.where(upper, steps[1] * state + beside, state)
    following = steps[0] * state + early
    own = jnp.where(core == 0, state, following)
    sent = jnp.where(core == 0, following, state)
    return own, ring(sent, [(i, i ^ 1) for i in range(count)])


def body(features, short_filter, mode_residue, decay_mix, skip_gain, counter, out_weight):
    rows = features.shape[0]
    channels = features.shape[2]
    count = lax.axis_size("ctx")
    tokens = rows * count
    index = lax.axis_index("ctx")
    side = lax.axis_index("ch")
    planes = jnp.transpose(features, (1, 0, 2))
    far_memory = lambda x: pltpu.with_memory_space_constraint(x, pltpu.HBM)
    edge = lax.ppermute(planes[:, rows - (SHORT - 1) :], "ctx", [(i, i + 1) for i in range(count - 1)])
    slot = jnp.arange(4, dtype=jnp.int32)

    def scalars(*values):
        out = jnp.zeros((4,), jnp.int32)
        for k, value in enumerate(values):
            out = jnp.where(slot == k, value, out)
        return out

    place = scalars(index * rows, side * channels, index % 2)
    to_send = scalars(1 - side, index % 2)
    to_keep = scalars(side, index % 2)
    gated, start, mine, other = gate(
        far_memory(counter), place, far_memory(planes), edge, far_memory(short_filter), far_memory(decay_mix), tokens
    )
    operands = (gated, planes, edge, short_filter, decay_mix, mode_residue, skip_gain[None], start)
    parts = [()]

    def between(piece):
        first, last = ((0, 2), (2, 3), (3, 4))[piece]
        parts[0] = local(to_send, operands, tokens, first, last, parts[0])

    own, got = states_before(mine, other, decay_mix, tokens, rows, index, count, between)
    sent = carry(to_send, parts[0], decay_mix, mode_residue, own, True, (), tokens)
    sent = carry(to_send, parts[0], decay_mix, mode_residue, got, False, (sent,), tokens)
    outs = out_weight.shape[1]
    received = []
    for first, cols in chunks_of(outs):
        part = project(sent, out_weight, first, cols, jnp.bfloat16)
        received.append(lax.ppermute(part, "ch", [(0, 1), (1, 0)]))
    own, part = lax.optimization_barrier((own, part))
    kept = blend(to_keep, operands, own, got, tokens)
    total = project(kept, out_weight, 0, outs, jnp.float32)
    done = ()
    for k, (first, _) in enumerate(chunks_of(outs)):
        done = (combine(total, received[k], first, done),)
    return done[0]


def solution(mesh):
    placed = (
        P(("dp", "ctx"), None, "ch"),
        P(None, None, "ch"),
        P(None, "ch"),
        P(None, "ch"),
        P("ch"),
        P("dp"),
        P("ch", None),
    )

    return jax.shard_map(body, mesh=mesh, in_specs=placed, out_specs=P(("dp", "ctx", "ch"), None), check_vma=False)
```

```python
import math

import jax
import jax.numpy as jnp
from jax import lax
from jax.experimental import pallas as pl
from jax.experimental.pallas import tpu as pltpu
from jax.sharding import PartitionSpec as P


SHORT = 3
ORDER = 16
LANES = 128
SUBS = 8
WIDTH = 2 * LANES
KEEP_SCALE = 8.0 / 7.0
TILE_COLS = 256
BASE = 40
GAP = 4
QUAD = 4
GATE_STEPS = 8


def rates_of(mix, length):
    return jnp.exp(-((1.0 - mix) * math.log(length) + mix * math.log(30.0)))


def row(table, index):
    return jnp.broadcast_to(table[index : index + 1, :], (SUBS, table.shape[1]))


def spread(rows, source, first, cols, count, step):
    for n in range(count):
        at = BASE + n * (step + GAP)
        spot = pl.ds(pl.multiple_of(first + n * step, step), step)
        rows[at : at + step, :] = source[spot, cols].astype(jnp.float32)


def across(rows, at, step):
    return rows[pl.ds(at, SUBS, stride=step + GAP), :]


def chunks_of(outs):
    sizes = [TILE_COLS] + [2 * TILE_COLS] * ((outs - TILE_COLS) // (2 * TILE_COLS))
    sizes += [TILE_COLS] * ((outs - sum(sizes)) // TILE_COLS)
    return [(sum(sizes[:k]), size) for k, size in enumerate(sizes)]


def lanes_of(group):
    return pl.ds(pl.multiple_of(group * LANES, LANES), LANES)


def state_of(own_ref, got_ref, core, group, groups):
    lanes = lanes_of(group % (groups // 2))
    return jnp.where(group // (groups // 2) == core, own_ref[:, lanes], got_ref[:, lanes])


def fill(table, values):
    for r in range(ORDER):
        table[r] = row(values, r)


def mask_kernel(half, step, counter, place, mask_ref):
    lane = lax.broadcasted_iota(jnp.int32, (SUBS, LANES), 1)
    sub = lax.broadcasted_iota(jnp.int32, (SUBS, LANES), 0)

    @pl.loop(0, mask_ref.shape[0])
    def _(group):
        channel = place[1] + group * LANES + lane
        for part in range(2):
            first = counter[1] + place[0] + part * half + sub * step
            bits = counter[0] + first * jnp.int32(-1640531535) + channel * jnp.int32(-2048144777)

            def several(j, bits):
                for u in range(GATE_STEPS):
                    h = bits + jnp.int32((-1640531535 * u + 2**31) % 2**32 - 2**31)
                    h = h ^ lax.shift_right_logical(h, jnp.full_like(h, 16))
                    h = h * jnp.int32(2146121005)
                    h = h ^ lax.shift_right_logical(h, jnp.full_like(h, 15))
                    h = h * jnp.int32(-2073254261)
                    keep = (h & jnp.int32(-536870912)) != 0
                    at = pl.multiple_of(part * half + (GATE_STEPS * j + u) * SUBS, SUBS)
                    mask_ref[group, pl.ds(at, SUBS), :] = jnp.where(keep, 1.0, 0.0)
                return bits + jnp.int32((-1640531535 * GATE_STEPS + 2**31) % 2**32 - 2**31)

            lax.fori_loop(0, step // GATE_STEPS, several, bits)


def totals_of(values, sub):
    for bit in (1, 2, 4):
        even = (sub & bit) == 0
        values = [
            jnp.where(even, a, b) + pltpu.roll(jnp.where(even, b, a), bit, 0)
            for a, b in zip(values[::2], values[1::2])
        ]
    return values[0]


def gate_kernel(tokens, half, step, place, mask_ref, key_ref, value_ref, edge_ref, taps_ref, mix_ref,
                gated_ref, start_ref, middle_ref, mine_ref, other_ref, key_rows, value_rows, decays, taps):
    block = pl.program_id(0)
    sub = lax.broadcasted_iota(jnp.int32, (SUBS, LANES), 0)
    later = ((SUBS - 1 - sub) * step).astype(jnp.float32)
    is_mine = (block * 2) // pl.num_programs(0) == place[2]
    for group in range(WIDTH // LANES):
        cols = slice(group * LANES, (group + 1) * LANES)
        place_of = block * (WIDTH // LANES) + group
        for rows, source, f in ((key_rows, key_ref, 1), (value_rows, value_ref, 2)):
            spread(rows, source, 0, cols, 2 * SUBS, step)
            rows[BASE - GAP - 2 : BASE - GAP, :] = edge_ref[f, :, lanes_of(place_of)].astype(jnp.float32)
        for lag in range(SHORT):
            taps[lag] = row(taps_ref[1, :, cols], lag) * KEEP_SCALE
            taps[SHORT + lag] = row(taps_ref[2, :, cols], lag)
        rates = rates_of(mix_ref[:, cols], tokens)
        fill(decays, jnp.exp(-rates))
        weights = [jnp.exp(-row(rates, r) * later) for r in range(ORDER)]
        ends = []
        for part in range(2):
            base = BASE + part * SUBS * (step + GAP)

            def quad(j, carry):
                states, k1, k2, v1, v2 = carry
                values = []
                for u in range(GATE_STEPS):
                    k0 = across(key_rows, base + GATE_STEPS * j + u, step)
                    v0 = across(value_rows, base + GATE_STEPS * j + u, step)
                    keyed = taps[0] * k0 + taps[1] * k1 + taps[2] * k2
                    valued = taps[3] * v0 + taps[4] * v1 + taps[5] * v2
                    at = pl.multiple_of(part * half + (GATE_STEPS * j + u) * SUBS, SUBS)
                    values.append(keyed * valued * mask_ref[place_of, pl.ds(at, SUBS), :])
                    k1, k2, v1, v2 = k0, k1, v0, v1
                wides = []
                for u in range(0, GATE_STEPS, 2):
                    rounded = jnp.concatenate(values[u : u + 2], axis=0).astype(jnp.bfloat16)
                    at = pl.multiple_of(part * half + (GATE_STEPS * j + u) * SUBS, 2 * SUBS)
                    gated_ref[place_of, pl.ds(at, 2 * SUBS), :] = rounded
                    wide = rounded.astype(jnp.float32)
                    wides += [wide[:SUBS], wide[SUBS:]]
                after = []
                for r, x in enumerate(states):
                    a = decays[r]
                    for g in wides:
                        x = x * a + g
                    after.append(x)
                return (tuple(after), k1, k2, v1, v2)

            zero = jnp.zeros((SUBS, LANES), jnp.float32)
            init = (
                (zero,) * ORDER,
                across(key_rows, base - GAP - 1, step),
                across(key_rows, base - GAP - 2, step),
                across(value_rows, base - GAP - 1, step),
                across(value_rows, base - GAP - 2, step),
            )
            states = lax.fori_loop(0, step // GATE_STEPS, quad, init)[0]
            for r in range(ORDER):
                start_ref[part, place_of, r] = states[r]
            weighted = [x * w for x, w in zip(states, weights)]
            ends.append(jnp.concatenate([totals_of(weighted[:SUBS], sub), totals_of(weighted[SUBS:], sub)], axis=0))
        middle_ref[:, lanes_of(place_of)] = ends[0]
        end = ends[1] + jnp.exp(-rates * float(half)) * ends[0]

        @pl.when(is_mine)
        def _():
            mine_ref[:, cols] = end

        @pl.when(jnp.logical_not(is_mine))
        def _():
            other_ref[:, cols] = end


def query_setup(tokens, half, step, which, lanes, planes_ref, edge_ref, taps_ref, mix_ref, query_rows, decays, taps):
    spread(query_rows, planes_ref.at[0], which * half, lanes, SUBS, step)
    tail = planes_ref[0, half - 2 * SUBS : half, lanes].astype(jnp.float32)[2 * SUBS - 2 :]
    edge = edge_ref[0, :, lanes].astype(jnp.float32)
    query_rows[BASE - GAP - 2 : BASE - GAP, :] = jnp.where(which == 0, edge, tail)
    for lag in range(SHORT):
        taps[lag] = row(taps_ref[0, :, lanes], lag)
    rates = rates_of(mix_ref[:, lanes], tokens)
    fill(decays, jnp.exp(-rates))
    return rates


def scan_quad(step, j, carry, gated_ref, base, query_rows, decays, gains, taps, skip, emit):
    states, q1, q2 = carry
    values = []
    for u in range(0, QUAD, 2):
        at = pl.multiple_of(base + (QUAD * j + u) * SUBS, 2 * SUBS)
        wide = gated_ref[pl.ds(at, 2 * SUBS), :].astype(jnp.float32)
        values += [wide[:SUBS], wide[SUBS:]]
    totals = [skip * g for g in values]
    after = []
    for r, x in enumerate(states):
        a = decays[r]
        c = gains[r]
        for u, g in enumerate(values):
            x = x * a + g
            totals[u] = totals[u] + x * c
        after.append(x)
    for u in range(QUAD):
        q0 = across(query_rows, BASE + QUAD * j + u, step)
        emit(u, taps[0] * q0 + taps[1] * q1 + taps[2] * q2, totals[u])
        q1, q2 = q0, q1
    return (tuple(after), q1, q2)


def states_in(start_ref, which, group, rates, into, step):
    sub = lax.broadcasted_iota(jnp.int32, (SUBS, LANES), 0)
    offset = (sub * step).astype(jnp.float32)
    jumps = {d: jnp.exp(-rates * float(d * step)) for d in (1, 2, 4)}
    states = []
    for r in range(ORDER):
        x = start_ref[which, group, r]
        for d in (1, 2, 4):
            x = x + row(jumps[d], r) * jnp.where(sub >= d, pltpu.roll(x, d, 0), 0.0)
        x = jnp.where(sub >= 1, pltpu.roll(x, 1, 0), 0.0)
        states.append(x + jnp.exp(-row(rates, r) * offset) * row(into, r))
    return tuple(states)


def gather(mixed_ref, mixed_rows, lanes, step):
    for n in range(SUBS):
        at = n * (step + GAP)
        mixed_ref[n * step : (n + 1) * step, lanes] = mixed_rows[at : at + step, :].astype(jnp.bfloat16)


def local_kernel(tokens, half, step, first, last, which, gated_ref, planes_ref, edge_ref, taps_ref, mix_ref,
                 residue_ref, skip_ref, start_ref, middle_ref, *rest):
    local_ref, filtered_ref, query_rows, decays, gains, taps = rest[-6:]

    @pl.loop(first, last)
    def _(group):
        lanes = lanes_of(group)
        rates = query_setup(tokens, half, step, which[0], lanes, planes_ref, edge_ref, taps_ref, mix_ref, query_rows, decays, taps)
        fill(gains, residue_ref[:, lanes])
        skip = row(skip_ref[:, lanes], 0)
        into = jnp.where(which[0] == 1, middle_ref[:, lanes], 0.0)

        def quad(j, carry):
            def emit(u, query, total):
                spot = pl.ds(pl.multiple_of((QUAD * j + u) * SUBS, SUBS), SUBS)
                local_ref[group, spot, :] = total
                filtered_ref[group, spot, :] = query

            return scan_quad(step, j, carry, gated_ref.at[group], which[0] * half, query_rows, decays, gains, taps, skip, emit)

        states = states_in(start_ref, which[0], group, rates, into, step)
        q1, q2 = across(query_rows, BASE - GAP - 1, step), across(query_rows, BASE - GAP - 2, step)
        lax.fori_loop(0, step // QUAD, quad, (states, q1, q2))


def blend_kernel(tokens, half, step, groups, which, gated_ref, planes_ref, edge_ref, taps_ref, mix_ref, residue_ref,
                 skip_ref, start_ref, middle_ref, own_ref, got_ref, mixed_ref, query_rows, decays, gains, taps, mixed_rows):
    @pl.loop(0, groups)
    def _(group):
        lanes = lanes_of(group)
        rates = query_setup(tokens, half, step, which[0], lanes, planes_ref, edge_ref, taps_ref, mix_ref, query_rows, decays, taps)
        fill(gains, residue_ref[:, lanes])
        skip = row(skip_ref[:, lanes], 0)
        into = state_of(own_ref, got_ref, which[1], group, groups)
        into = jnp.where(which[0] == 1, jnp.exp(-rates * float(half)) * into + middle_ref[:, lanes], into)

        def quad(j, carry):
            def emit(u, query, total):
                mixed_rows[pl.ds(QUAD * j + u, SUBS, stride=step + GAP), :] = query * total

            return scan_quad(step, j, carry, gated_ref.at[group], which[0] * half, query_rows, decays, gains, taps, skip, emit)

        states = states_in(start_ref, which[0], group, rates, into, step)
        q1, q2 = across(query_rows, BASE - GAP - 1, step), across(query_rows, BASE - GAP - 2, step)
        lax.fori_loop(0, step // QUAD, quad, (states, q1, q2))
        gather(mixed_ref, mixed_rows, lanes, step)


def carry_kernel(tokens, half, step, groups, mine, which, local_ref, filtered_ref, mix_ref, residue_ref, state_ref, *rest):
    mixed_ref, decays, mixed_rows = rest[-3:]
    sub = lax.broadcasted_iota(jnp.int32, (SUBS, LANES), 0)
    offset = (which[0] * half + sub * step + 1).astype(jnp.float32)

    base = (which[1] if mine else 1 - which[1]) * groups

    @pl.loop(0, groups)
    def _(at):
        group = base + at
        lanes = lanes_of(group)
        rates = rates_of(mix_ref[:, lanes], tokens)
        fill(decays, jnp.exp(-rates))
        into = state_ref[:, lanes_of(at)] * residue_ref[:, lanes]

        def quad(j, states):
            totals = [None] * QUAD
            after = []
            for r, x in enumerate(states):
                a = decays[r]
                for u in range(QUAD):
                    totals[u] = x if totals[u] is None else totals[u] + x
                    x = x * a
                after.append(x)
            for u in range(QUAD):
                spot = pl.ds(pl.multiple_of((QUAD * j + u) * SUBS, SUBS), SUBS)
                value = filtered_ref[group, spot, :] * (local_ref[group, spot, :] + totals[u])
                mixed_rows[pl.ds(QUAD * j + u, SUBS, stride=step + GAP), :] = value
            return tuple(after)

        states = tuple(jnp.exp(-row(rates, r) * offset) * row(into, r) for r in range(ORDER))
        lax.fori_loop(0, step // QUAD, quad, states)
        gather(mixed_ref, mixed_rows, lanes, step)


def project_kernel(mixed_ref, weight_ref, out_ref):
    out_ref[...] = jnp.dot(mixed_ref[...], weight_ref[...], preferred_element_type=jnp.float32).astype(out_ref.dtype)


def combine_kernel(own_ref, got_ref, *rest):
    lanes = pl.ds(pl.multiple_of(pl.program_id(0) * TILE_COLS, TILE_COLS), TILE_COLS)
    rest[-1][...] = (own_ref[...] + got_ref[:, lanes].astype(jnp.float32)).astype(jnp.bfloat16)


def table(count=ORDER):
    return pltpu.VMEM((count, SUBS, LANES), jnp.float32)


def room(mib):
    return pltpu.CompilerParams(vmem_limit_bytes=mib * 2**20)


def cost(vectors, moved):
    return pl.CostEstimate(flops=vectors, bytes_accessed=moved, transcendentals=0)


def mask_of(counter, place, rows, channels):
    half = rows // 2
    return pl.pallas_call(
        lambda *refs: mask_kernel(half, half // SUBS, *refs),
        out_shape=pltpu.VMEM((channels // LANES, rows, LANES), jnp.float32),
        grid_spec=pltpu.PrefetchScalarGridSpec(
            num_scalar_prefetch=2, grid=(1,), in_specs=[], out_specs=pl.BlockSpec(memory_space=pltpu.VMEM)
        ),
        name="mask",
        compiler_params=room(16),
        cost_estimate=cost(2 * 10**9, 2**20),
    )(counter, place)


def gate(place, mask, planes, edge, taps, mix, tokens):
    rows, channels = planes.shape[1:]
    half = rows // 2
    step = half // SUBS
    blocks = channels // WIDTH
    spread_rows = 2 * BASE + 2 * SUBS * (step + GAP)
    first = lambda b, owner: jnp.clip(b - owner * (blocks // 2), 0, blocks // 2 - 1)
    return pl.pallas_call(
        lambda *refs: gate_kernel(tokens, half, step, *refs),
        out_shape=(
            pltpu.VMEM((channels // LANES, rows, LANES), jnp.bfloat16),
            pltpu.VMEM((2, channels // LANES, ORDER, SUBS, LANES), jnp.float32),
            pltpu.VMEM((ORDER, channels), jnp.float32),
            jax.ShapeDtypeStruct((ORDER, channels // 2), jnp.float32),
            jax.ShapeDtypeStruct((ORDER, channels // 2), jnp.float32),
        ),
        grid_spec=pltpu.PrefetchScalarGridSpec(
            num_scalar_prefetch=1,
            grid=(blocks,),
            in_specs=[
                pl.BlockSpec(memory_space=pltpu.VMEM),
                pl.BlockSpec((None, rows, WIDTH), lambda b, s: (1, 0, b)),
                pl.BlockSpec((None, rows, WIDTH), lambda b, s: (2, 0, b)),
                pl.BlockSpec(memory_space=pltpu.VMEM),
                pl.BlockSpec((3, SHORT, WIDTH), lambda b, s: (0, 0, b)),
                pl.BlockSpec((ORDER, WIDTH), lambda b, s: (0, b)),
            ],
            out_specs=(
                pl.BlockSpec(memory_space=pltpu.VMEM),
                pl.BlockSpec(memory_space=pltpu.VMEM),
                pl.BlockSpec(memory_space=pltpu.VMEM),
                pl.BlockSpec((ORDER, WIDTH), lambda b, s: (0, first(b, s[2]))),
                pl.BlockSpec((ORDER, WIDTH), lambda b, s: (0, first(b, 1 - s[2]))),
            ),
            scratch_shapes=[pltpu.VMEM((spread_rows, LANES), jnp.float32)] * 2 + [table(), table(2 * SHORT)],
        ),
        name="gate",
        compiler_params=room(16),
        cost_estimate=cost(11 * 10**9, 4 * rows * channels),
    )(place, mask, planes, planes, edge, taps, mix)


def scan_scratch(step):
    return [pltpu.VMEM((2 * BASE + SUBS * (step + GAP), LANES), jnp.float32), table(), table(), table(SHORT)]


def resident(kernel, which, operands, out_shape, scratch, aliases, time):
    several = isinstance(out_shape, tuple)
    place = pl.BlockSpec(memory_space=pltpu.VMEM)
    return pl.pallas_call(
        kernel,
        out_shape=out_shape,
        grid_spec=pltpu.PrefetchScalarGridSpec(
            num_scalar_prefetch=1,
            grid=(1,),
            in_specs=[place] * len(operands),
            out_specs=(place,) * len(out_shape) if several else place,
            scratch_shapes=scratch,
        ),
        input_output_aliases=aliases,
        compiler_params=room(16),
        cost_estimate=cost(int(time * 10**9), 2**20),
    )(which, *operands)


def local(which, operands, tokens, first, last, before):
    groups, rows = operands[0].shape[:2]
    half = rows // 2
    step = half // SUBS
    shape = pltpu.VMEM((groups, half, LANES), jnp.float32)
    first, last = first * groups // 4, last * groups // 4
    return resident(
        lambda *refs: local_kernel(tokens, half, step, first, last, *refs), which, (*operands, *before), (shape, shape),
        scan_scratch(step), {1 + len(operands) + k: k for k in range(len(before))}, 0.55 * (last - first),
    )


def carry(which, parts, mix, residue, state, mine, before, tokens):
    groups, half = parts[0].shape[:2]
    step = half // SUBS
    return resident(
        lambda *refs: carry_kernel(tokens, half, step, groups // 2, mine, *refs), which,
        (*parts, mix, residue, state, *before), pltpu.VMEM((half, groups * LANES), jnp.bfloat16),
        [table(), pltpu.VMEM((2 * BASE + SUBS * (step + GAP), LANES), jnp.float32)], {6: 0} if before else {}, 2.5,
    )


def blend(which, operands, own, got, tokens):
    groups, rows = operands[0].shape[:2]
    half = rows // 2
    step = half // SUBS
    return resident(
        lambda *refs: blend_kernel(tokens, half, step, groups, *refs), which, (*operands, own, got),
        jax.ShapeDtypeStruct((half, groups * LANES), jnp.bfloat16),
        scan_scratch(step) + [pltpu.VMEM((2 * BASE + SUBS * (step + GAP), LANES), jnp.float32)], {}, 9,
    )


def project(mixed, weight, first, cols, dtype):
    rows, depth = mixed.shape
    at = first // TILE_COLS
    return pl.pallas_call(
        project_kernel,
        out_shape=jax.ShapeDtypeStruct((rows, cols), dtype),
        grid=(cols // TILE_COLS,),
        in_specs=[
            pl.BlockSpec((rows, depth), lambda n: (0, 0)),
            pl.BlockSpec((depth, TILE_COLS), lambda n: (0, at + n)),
        ],
        out_specs=pl.BlockSpec((rows, TILE_COLS), lambda n: (0, n)),
        compiler_params=room(16),
        cost_estimate=cost(2 * rows * depth * cols, 2 * (rows * depth + depth * cols)),
    )(mixed, weight)


def combine(own, got, first, before):
    rows, cols = got.shape
    at = first // TILE_COLS
    block = pl.BlockSpec((rows, TILE_COLS), lambda n: (0, at + n))
    return pl.pallas_call(
        combine_kernel,
        out_shape=jax.ShapeDtypeStruct(own.shape, jnp.bfloat16),
        grid=(cols // TILE_COLS,),
        in_specs=[block, pl.BlockSpec(memory_space=pltpu.VMEM)]
        + [pl.BlockSpec(memory_space=pl.ANY)] * len(before),
        out_specs=block,
        input_output_aliases={2: 0} if before else {},
        name="combine",
        compiler_params=room(8),
        cost_estimate=cost(rows * cols, 8 * rows * cols),
    )(own, got, *before)


def states_before(mine, other, mix, tokens, rows, index, count, between):
    core = index % 2
    width = mine.shape[1]
    rates = rates_of(lax.dynamic_slice_in_dim(mix, core * width, width, 1), tokens)
    decay = lambda chunks: jnp.exp(-rates * float(rows * chunks))
    steps = [decay(n) for n in (1, 2, 4)]
    assert count == 16

    def ring(value, pairs):
        return lax.ppermute(value, "ctx", pairs)

    sibling = ring(other, [(i, i ^ 1) for i in range(count)])
    early = jnp.where(core == 0, mine, sibling)
    late = jnp.where(core == 0, sibling, mine)
    chip = steps[0] * early + late
    beside = ring(chip, [(i, i ^ 2) for i in range(count)])
    between(0)
    upper = (index // 2) % 2 == 1
    group = jnp.where(upper, steps[1] * beside + chip, steps[1] * chip + beside)
    ring_at = index // 4
    odd = ring_at % 2 == 1
    near = ring(group, [(i, i ^ 4) for i in range(count)])
    between(1)
    couple = jnp.where(odd, steps[2] * near + group, steps[2] * group + near)
    far = ring(couple, [(i, (3 - i // 4) * 4 + i % 4) for i in range(count)])
    between(2)
    state = jnp.where(ring_at >= 2, jnp.where(odd, steps[2] * far, far), 0.0) + jnp.where(odd, near, 0.0)
    state = jnp.where(upper, steps[1] * state + beside, state)
    following = steps[0] * state + early
    own = jnp.where(core == 0, state, following)
    sent = jnp.where(core == 0, following, state)
    return own, ring(sent, [(i, i ^ 1) for i in range(count)])


def body(features, short_filter, mode_residue, decay_mix, skip_gain, counter, out_weight):
    rows = features.shape[0]
    channels = features.shape[2]
    count = lax.axis_size("ctx")
    tokens = rows * count
    index = lax.axis_index("ctx")
    side = lax.axis_index("ch")
    planes = jnp.transpose(features, (1, 0, 2))
    far_memory = lambda x: pltpu.with_memory_space_constraint(x, pltpu.HBM)
    edge = lax.ppermute(planes[:, rows - (SHORT - 1) :], "ctx", [(i, i + 1) for i in range(count - 1)])
    slot = jnp.arange(4, dtype=jnp.int32)

    def scalars(*values):
        out = jnp.zeros((4,), jnp.int32)
        for k, value in enumerate(values):
            out = jnp.where(slot == k, value, out)
        return out

    place = scalars(index * rows, side * channels, index % 2)
    to_send = scalars(1 - side, index % 2)
    to_keep = scalars(side, index % 2)
    mask = mask_of(far_memory(counter), place, rows, channels)
    gated, start, middle, mine, other = gate(
        place, mask, far_memory(planes), edge, far_memory(short_filter), far_memory(decay_mix), tokens
    )
    operands = (gated, planes, edge, short_filter, decay_mix, mode_residue, skip_gain[None], start, middle)
    parts = [()]

    def between(piece):
        first, last = ((0, 2), (2, 3), (3, 4))[piece]
        parts[0] = local(to_send, operands, tokens, first, last, parts[0])

    own, got = states_before(mine, other, decay_mix, tokens, rows, index, count, between)
    sent = carry(to_send, parts[0], decay_mix, mode_residue, own, True, (), tokens)
    sent = carry(to_send, parts[0], decay_mix, mode_residue, got, False, (sent,), tokens)
    outs = out_weight.shape[1]
    received = []
    for first, cols in chunks_of(outs):
        part = project(sent, out_weight, first, cols, jnp.bfloat16)
        received.append(lax.ppermute(part, "ch", [(0, 1), (1, 0)]))
    own, part = lax.optimization_barrier((own, part))
    kept = blend(to_keep, operands, own, got, tokens)
    total = project(kept, out_weight, 0, outs, jnp.float32)
    done = ()
    for k, (first, _) in enumerate(chunks_of(outs)):
        done = (combine(total, received[k], first, done),)
    return done[0]


def solution(mesh):
    placed = (
        P(("dp", "ctx"), None, "ch"),
        P(None, None, "ch"),
        P(None, "ch"),
        P(None, "ch"),
        P("ch"),
        P("dp"),
        P("ch", None),
    )

    return jax.shard_map(body, mesh=mesh, in_specs=placed, out_specs=P(("dp", "ctx", "ch"), None), check_vma=False)
```
